32 devices in a mesh: groups: 2 (over y), dp: 4 (over z), kv: 4 (over x, core).
Axes of the slice: x: 2, y: 2, z: 4, core: 2. Of those that a mesh axis runs over, the one named last changes fastest.
Arguments:
- queries: bfloat16 [128, 3, 8192], P(('groups', 'dp'), None, 'kv'), parts along dimension 0, may hold values from -12 to 12
- routes: int32 [128, 1], P(('groups', 'dp')), parts along dimension 0, may hold values from 0 to 3; in each aligned block of 16 rows (0 to 15, 16 to 31, ...) at most 8 rows name the same one
- suffix_lengths: int32 [128], P(('groups', 'dp')), parts along dimension 0, may hold values from 128 to 256
- prefix_keys: bfloat16 [8, 2048, 1024], P(('groups', 'dp'), None, 'kv'), parts along dimension 0, may hold values from -8 to 8
- prefix_values: bfloat16 [8, 2048, 1024], P(('groups', 'dp'), None, 'kv'), parts along dimension 0, may hold values from -4.5 to 4.5
- suffix_keys: bfloat16 [128, 256, 1024], P(('groups', 'dp'), None, 'kv'), parts along dimension 0, may hold values from -4.5 to 4.5
- suffix_values: bfloat16 [128, 256, 1024], P(('groups', 'dp'), None, 'kv'), parts along dimension 0, may hold values from -4.5 to 4.5
- new_keys: bfloat16 [128, 3, 1024], P(('groups', 'dp'), None, 'kv'), parts along dimension 0, may hold values from -4.5 to 4.5
- new_values: bfloat16 [128, 3, 1024], P(('groups', 'dp'), None, 'kv'), parts along dimension 0, may hold values from -4.5 to 4.5
- out_weight: bfloat16 [8192, 8192], P('kv', 'dp'), may hold values from -0.0625 to 0.0625
Outputs:
- projected: bfloat16 [128, 3, 8192], P(('groups', 'kv'), None, 'dp'), parts along dimension 0
The draws below stay inside these ranges and needn't reach their ends.
There are 2 independent parts, one for each index of `groups`. The reference program is written for one: setup_inputs(seed, part) draws one part's arguments, and reference() takes and returns one part's arrays. A program takes and returns all parts, laid end to end along the dimension named above; an argument that names none is the same for every part. Nothing has to cross between parts.
Inputs may be any that keep to these rules, and one draw needn't show every extreme that they name: `routes`: among the 16 candidates of one index of dp at most 8 continue the same prompt, and in every draw some prompt receives exactly 8 of them from some index.
All inputs are finite; a program needn't handle non-finite values.
Results may differ from the reference program's by a relative error of at most 0.008.
Values may be sent and summed in bfloat16 or wider, within the bound.
A program may use at most 128 MiB of HBM per device.

```python
import math
import jax
import jax.numpy as jnp
import numpy as np
from jax import lax

D = 8192
QHEADS = 64
KVH = 8
HD = 128
PLEN = 2048
SUF = 256
CAND_DEV = 16
STEPS = 3
PROMPTS = 4
CANDS = 64
CAP = 8


def draw_prefix_keys(key, part):
    main_key = jax.random.fold_in(key, 11)
    full_shape = (PROMPTS, PLEN, KVH * HD)
    drawn = jnp.clip(jax.random.normal(main_key, full_shape, jnp.float32), -4.5, 4.5)
    return drawn.astype(jnp.bfloat16)


def draw_suffix_keys(key, part):
    main_key = jax.random.fold_in(key, 31)
    full_shape = (CANDS, SUF, KVH * HD)
    drawn = jnp.clip(jax.random.normal(main_key, full_shape, jnp.float32), -4.5, 4.5)
    return drawn.astype(jnp.bfloat16)


def draw_queries(key, part):
    main_key = jax.random.fold_in(key, 21)
    full_shape = (CANDS, STEPS, QHEADS * HD)
    drawn = jnp.clip(3.0 * jax.random.normal(main_key, full_shape, jnp.float32), -12.0, 12.0)
    return drawn.astype(jnp.bfloat16)


def plant(result, rng, smallest, largest):
    longest = result.shape.index(max(result.shape))
    spots = []
    for shift in (0, 1):
        where = [jax.random.randint(jax.random.fold_in(rng, axis), (), 0, length) for axis, length in enumerate(result.shape)]
        where[longest] = (where[longest] + shift) % result.shape[longest]
        spots.append(tuple(where))
    return result.at[spots[0]].set(smallest).at[spots[1]].set(largest)


def shard_levels(own_key, extent, shards, low, high):
    def one(axis_at, parts):
        steps = jax.random.uniform(jax.random.fold_in(jax.random.fold_in(own_key, 6), axis_at), (parts,), jnp.float32, low / len(shards), high / len(shards))
        return jnp.repeat(jnp.exp(steps), extent[axis_at] // parts).reshape((-1,) + (1,) * (len(extent) - axis_at - 1))

    loudness = one(*shards[0])
    for cut in shards[1:]:
        loudness = loudness * one(*cut)
    return loudness


def assign_block(stream_key, own, number, rows, amount, top, limit, skew):
    order = jax.random.permutation(stream_key, amount)
    crowded, usual = load_shares(amount, rows * top, limit, skew, True), load_shares(amount, rows * top, limit, skew, False)
    places = jnp.arange(amount)

    def named(tallies, rotation):
        used = int((tallies > 0).sum())
        fixed = max(1, used // 4)
        passed = fixed + (places - fixed + rotation * (used - fixed)) % max(1, amount - fixed)
        return jnp.zeros((amount,), jnp.int32).at[order[jnp.where(places < fixed, places, passed)]].set(jnp.asarray(tallies, jnp.int32))

    tallies = jnp.where(number % 4 == 0, named(crowded, number // 4), named(usual, number - number // 4 - 1))
    mixed = jax.random.permutation(jax.random.fold_in(own, 3), amount)
    giver, receiver = mixed[0:amount // 2 * 2:2], mixed[1:amount // 2 * 2:2]
    margin = jnp.minimum(tallies[giver] - 1, limit - tallies[receiver]) // 2
    margin = jnp.where((giver == order[0]) | (receiver == order[0]) | (tallies[receiver] == 0), 0, jnp.maximum(margin, 0))
    passed = jax.random.randint(jax.random.fold_in(own, 4), (amount // 2,), 0, 1 << 20) % (margin + 1)
    tallies = tallies.at[giver].add(-passed).at[receiver].add(passed)
    members = jnp.searchsorted(jnp.cumsum(tallies), jnp.arange(rows * top), side="right").astype(jnp.int32)
    grid = members.reshape(top, rows).T
    grid = grid[jax.random.permutation(jax.random.fold_in(own, 1), rows)]
    rotation = jax.random.randint(jax.random.fold_in(own, 2), (rows, 1), 0, top)
    return jnp.take_along_axis(grid, (jnp.arange(top)[None, :] + rotation) % top, axis=1)


def load_shares(number_of, total, limit, skew, full):
    loads = [(1 << 20) // math.isqrt(rank ** skew) + 1 for rank in range(1, number_of + 1)]
    largest = limit if full else min(limit, max(-(-total // number_of), total * loads[0] // sum(loads)))
    least = 1 if total - largest >= number_of - 1 else 0
    holding, rest = [largest] + [least] * (number_of - 1), total - largest - least * (number_of - 1)
    while rest > 0:
        free = [i for i in range(1, number_of) if holding[i] < largest] or [i for i in range(1, number_of) if holding[i] < limit]
        pool, remaining = sum([loads[i] for i in free]), rest
        for i in free:
            addition = min(limit - holding[i], max(1, remaining * loads[i] // pool), rest)
            holding[i] = holding[i] + addition
            rest = rest - addition
    return np.array(holding)


def normal_values(own_key, extent, deviation, limit, split=(), kind=jnp.bfloat16):
    values = deviation * jax.random.normal(own_key, extent, jnp.float32)
    if split:
        values = values * shard_levels(own_key, extent, split, -0.22, 0.18)
    return jnp.clip(values, -limit, limit).astype(kind)


def setup_inputs(seed: int = 0, part: int = 0) -> dict:
    arg_keys = jax.random.split(jax.random.key(seed), 11)
    part_splits = jax.random.split(jax.random.fold_in(arg_keys[10], part), 11)
    queries = draw_queries(jax.random.fold_in(jax.random.fold_in(arg_keys[10], part), 71), part)
    routes_keys = jax.random.split(jax.random.fold_in(part_splits[1], 1), CANDS // CAND_DEV)
    routes_turns = jax.random.permutation(jax.random.fold_in(part_splits[1], 3), CANDS // CAND_DEV)
    routes = jax.vmap(lambda own, number: assign_block(jax.random.fold_in(part_splits[1], 2), own, number, CAND_DEV, PROMPTS, 1, CAP, 2))(routes_keys, routes_turns).reshape((CANDS, 1))
    suffix_lengths = plant(jax.random.randint(part_splits[2], (CANDS,), SUF // 2, SUF + 1), jax.random.fold_in(part_splits[2], 1), SUF // 2, SUF).astype(jnp.int32)
    prefix_keys = draw_prefix_keys(jax.random.fold_in(jax.random.fold_in(arg_keys[10], part), 71), part)
    prefix_values = normal_values(part_splits[4], (PROMPTS, PLEN, KVH * HD), 1.0, 4.5, ((0, 4), (2, 4)))
    suffix_keys = draw_suffix_keys(jax.random.fold_in(jax.random.fold_in(arg_keys[10], part), 71), part)
    suffix_values = normal_values(part_splits[6], (CANDS, SUF, KVH * HD), 1.0, 4.5, ((0, 4), (2, 4)))
    new_keys = normal_values(part_splits[7], (CANDS, STEPS, KVH * HD), 1.0, 4.5, ((0, 4), (2, 4)))
    new_values = normal_values(part_splits[8], (CANDS, STEPS, KVH * HD), 1.0, 4.5, ((0, 4), (2, 4)))
    out_weight = normal_values(arg_keys[9], (QHEADS * HD, D), (QHEADS * HD) ** -0.5, 0.0625, ((0, 4), (1, 4)))
    return {"queries": queries, "routes": routes, "suffix_lengths": suffix_lengths, "prefix_keys": prefix_keys, "prefix_values": prefix_values, "suffix_keys": suffix_keys, "suffix_values": suffix_values, "new_keys": new_keys, "new_values": new_values, "out_weight": out_weight}


def reference(queries, routes, suffix_lengths, prefix_keys, prefix_values, suffix_keys, suffix_values, new_keys, new_values, out_weight):
    group_size = QHEADS // KVH
    score_scale = 1.0 / math.sqrt(HD)
    cache_positions = jnp.arange(SUF, dtype=jnp.int32)
    step_positions = jnp.arange(STEPS, dtype=jnp.int32)
    new_allowed = step_positions[None, :] <= step_positions[:, None]

    def attend(candidate):
        query_rows, owner_index, length, cache_keys, cache_values, fresh_keys, fresh_values = candidate
        prompt_keys = lax.dynamic_index_in_dim(prefix_keys, owner_index.astype(jnp.int32), 0, keepdims=False)
        prompt_values = lax.dynamic_index_in_dim(prefix_values, owner_index.astype(jnp.int32), 0, keepdims=False)
        key_rows = jnp.concatenate([prompt_keys, cache_keys, fresh_keys], 0).astype(jnp.float32).reshape(-1, KVH, HD)
        value_rows = jnp.concatenate([prompt_values, cache_values, fresh_values], 0).astype(jnp.float32).reshape(-1, KVH, HD)
        query_heads = query_rows.astype(jnp.float32).reshape(STEPS, KVH, group_size, HD)
        scores = jnp.einsum('shgd,khd->shgk', query_heads, key_rows) * score_scale
        allowed = jnp.concatenate([jnp.ones((STEPS, PLEN), dtype=bool), jnp.broadcast_to(cache_positions[None, :] < length, (STEPS, SUF)), new_allowed], 1)
        scores = jnp.where(allowed[:, None, None, :], scores, -jnp.inf)
        peak_score = lax.optimization_barrier(jnp.max(scores, -1, keepdims=True))
        weights = jnp.exp(scores - peak_score)
        weight_sum = lax.optimization_barrier(jnp.sum(weights, -1, keepdims=True))
        combined = jnp.einsum('shgk,khd->shgd', weights / weight_sum, value_rows)
        return combined.reshape(STEPS, QHEADS * HD).astype(jnp.bfloat16)
    attended = lax.map(attend, (queries, routes[:, 0], suffix_lengths, suffix_keys, suffix_values, new_keys, new_values))
    projected = jnp.dot(attended.reshape(CANDS * STEPS, QHEADS * HD), out_weight, preferred_element_type=jnp.float32)
    return projected.reshape(CANDS, STEPS, D).astype(jnp.bfloat16)
```

```python
import functools
import math

import jax
import jax.numpy as jnp
from jax import lax
from jax.experimental import pallas as pl
from jax.experimental.pallas import tpu as pltpu
from jax.sharding import PartitionSpec as P

HD = 128
MESH = pl.DeviceIdType.MESH
NEG = -1e30


def kernel(
    n,
    n_kv,
    cap,
    slot_ref,
    inv_ref,
    len_ref,
    q_ref,
    nk_ref,
    nv_ref,
    pk_hbm,
    pv_hbm,
    sk_hbm,
    sv_hbm,
    w_hbm,
    o_ref,
    kbuf,
    vbuf,
    skbuf,
    svbuf,
    wbuf,
    qsend,
    qrecv,
    suf_o,
    suf_l,
    psend_o,
    psend_l,
    precv_o,
    precv_l,
    att,
    gath,
    ysend,
    red,
    own,
    local_sem,
    q_ss,
    q_rs,
    po_ss,
    po_rs,
    pl_ss,
    pl_rs,
    g_ss,
    g_rs,
    y_ss,
    y_rs,
):
    f32, bf16 = jnp.float32, jnp.bfloat16
    me = lax.axis_index("dp")
    kv = lax.axis_index("kv")
    cands, steps, heads, _ = q_ref.shape
    kv_heads = kbuf.shape[1] // HD
    group = heads // kv_heads
    rows = cands * steps
    gc = n // n_kv
    cols = wbuf.shape[1]
    scale = 1.0 / math.sqrt(HD)

    loads = [
        pltpu.make_async_copy(src, dst, local_sem.at[i])
        for i, (src, dst) in enumerate(
            [(sk_hbm, skbuf), (sv_hbm, svbuf), (pk_hbm, kbuf), (pv_hbm, vbuf), (w_hbm, wbuf)]
        )
    ]
    for load in loads:
        load.start()

    barrier = pltpu.get_barrier_semaphore()

    @pl.loop(1, n)
    def _(k):
        pl.semaphore_signal(
            barrier, inc=1, device_id={"dp": lax.rem(me + k, n)}, device_id_type=MESH
        )

    @pl.loop(1, n_kv)
    def _(k):
        pl.semaphore_signal(
            barrier, inc=1, device_id={"kv": lax.rem(kv + k, n_kv)}, device_id_type=MESH
        )

    @pl.loop(0, n)
    def _(k):
        for j in range(cap):
            qsend[k, j] = q_ref[inv_ref[k * cap + j]]

    qrecv[0] = qsend[0]
    pl.semaphore_wait(barrier, n - 1 + n_kv - 1)

    def q_copy(k):
        return pltpu.make_async_remote_copy(
            src_ref=qsend.at[k],
            dst_ref=qrecv.at[k],
            send_sem=q_ss.at[k],
            recv_sem=q_rs.at[k],
            device_id={"dp": lax.rem(me + k, n)},
            device_id_type=MESH,
        )

    def po_copy(k):
        return pltpu.make_async_remote_copy(
            src_ref=psend_o.at[k],
            dst_ref=precv_o.at[pl.ds(k * cap, cap)],
            send_sem=po_ss.at[k],
            recv_sem=po_rs.at[k],
            device_id={"dp": lax.rem(me + n - k, n)},
            device_id_type=MESH,
        )

    def pl_copy(k):
        return pltpu.make_async_remote_copy(
            src_ref=psend_l.at[k],
            dst_ref=precv_l.at[pl.ds(k * cap, cap)],
            send_sem=pl_ss.at[k],
            recv_sem=pl_rs.at[k],
            device_id={"dp": lax.rem(me + n - k, n)},
            device_id_type=MESH,
        )

    def g_copy(k):
        return pltpu.make_async_remote_copy(
            src_ref=gath.at[0],
            dst_ref=gath.at[k],
            send_sem=g_ss.at[k],
            recv_sem=g_rs.at[k],
            device_id={"dp": lax.rem(me + k, n)},
            device_id_type=MESH,
        )

    @pl.loop(1, n)
    def _(k):
        q_copy(k).start()

    loads[0].wait()
    loads[1].wait()
    depth = skbuf.shape[1]
    position = lax.broadcasted_iota(jnp.int32, (steps * group, depth), 1)
    step_of = lax.broadcasted_iota(jnp.int32, (steps, group, 1), 0).reshape(steps * group, 1)

    def suffix(c):
        q = q_ref[c].astype(f32)
        fresh_k = nk_ref[c].astype(f32)
        fresh_v = nv_ref[c].astype(f32)
        length = len_ref[c]
        outs, totals = [], []
        for h in range(kv_heads):
            lanes = slice(h * HD, (h + 1) * HD)
            qh = q[:, h * group : (h + 1) * group, :].reshape(steps * group, HD)
            s = lax.dot_general(
                qh.astype(bf16),
                skbuf[c, :, lanes],
                (((1,), (1,)), ((), ())),
                preferred_element_type=f32,
            )
            s = jnp.where(position < length, s * scale, NEG)
            top = jnp.max(s, 1, keepdims=True)
            news = []
            for t in range(steps):
                f = jnp.sum(qh * fresh_k[t : t + 1, lanes], 1, keepdims=True) * scale
                f = jnp.where(step_of >= t, f, NEG)
                top = jnp.maximum(top, f)
                news.append(f)
            p = jnp.exp(s - top)
            total = jnp.sum(p, 1, keepdims=True)
            o = jnp.dot(p.astype(bf16), svbuf[c, :, lanes], preferred_element_type=f32)
            for t in range(steps):
                e = jnp.exp(news[t] - top)
                total = total + e
                o = o + e * fresh_v[t : t + 1, lanes]
            outs.append((o / total).reshape(steps, group, HD))
            totals.append(
                jnp.broadcast_to(top + jnp.log(total), (steps * group, HD)).reshape(
                    steps, group, HD
                )
            )
        suf_o[c] = jnp.concatenate(outs, 1)
        suf_l[c] = jnp.concatenate(totals, 1)

    together = 4 if cands % 4 == 0 else 1

    @pl.loop(0, cands // together)
    def _(i):
        for u in range(together):
            suffix(i * together + u)

    loads[2].wait()
    loads[3].wait()
    lane = lax.broadcasted_iota(jnp.int32, (1, group, HD), 2)
    sub = lax.broadcasted_iota(jnp.int32, (1, group, HD), 1)

    @pl.loop(0, n)
    def _(k):
        @pl.when(k > 0)
        def _():
            q_copy(k).wait_recv()

        x = qrecv[k].astype(f32).reshape(cap * steps, heads, HD)
        outs, packed = [], None
        for h in range(kv_heads):
            lanes = slice(h * HD, (h + 1) * HD)
            xh = x[:, h * group : (h + 1) * group, :].reshape(cap * steps * group, HD)
            s = (
                lax.dot_general(
                    xh.astype(bf16),
                    kbuf[:, lanes],
                    (((1,), (1,)), ((), ())),
                    preferred_element_type=f32,
                )
                * scale
            )
            top = jnp.max(s, 1, keepdims=True)
            p = jnp.exp(s - top)
            total = jnp.sum(p, 1, keepdims=True)
            o = jnp.dot(p.astype(bf16), vbuf[:, lanes], preferred_element_type=f32) / total
            outs.append(o.reshape(cap * steps, group, HD))
            lse = jnp.broadcast_to(top + jnp.log(total), (cap * steps * group, HD))
            lse = lse.reshape(cap * steps, group, HD)
            lse = jnp.sum(jnp.where(lane == sub + h * group, lse, 0.0), 1)
            packed = lse if packed is None else packed + lse
        o = jnp.concatenate(outs, 1).astype(bf16).reshape(cap, steps, heads, HD)
        packed = packed.reshape(cap, steps, HD)

        @pl.when(k == 0)
        def _():
            precv_o[0:cap] = o
            precv_l[0:cap] = packed

        @pl.when(k > 0)
        def _():
            psend_o[k] = o
            psend_l[k] = packed
            po_copy(k).start()
            pl_copy(k).start()

    @pl.loop(1, n)
    def _(k):
        po_copy(k).wait_recv()
        pl_copy(k).wait_recv()

    diag = lax.broadcasted_iota(jnp.int32, (steps, heads, HD), 2) == lax.broadcasted_iota(
        jnp.int32, (steps, heads, HD), 1
    )

    @pl.loop(0, cands)
    def _(c):
        slot = slot_ref[c]
        pr = precv_o[slot].astype(f32)
        pt = jnp.broadcast_to(precv_l[slot].reshape(steps, 1, HD), (steps, heads, HD))
        pt = jnp.sum(jnp.where(diag, pt, 0.0), 2, keepdims=True)
        st = suf_l[c]
        peak = jnp.maximum(pt, st)
        a = jnp.exp(pt - peak)
        b = jnp.exp(st - peak)
        merged = (a * pr + b * suf_o[c]) / (a + b)
        att[pl.ds(pl.multiple_of(c * steps * heads, 8), steps * heads), :] = merged.reshape(
            steps * heads, HD
        )

    for hg in range(heads):
        gath[0, :, hg * HD : (hg + 1) * HD] = att[pl.ds(hg, rows, stride=heads), :].astype(bf16)

    @pl.loop(1, n)
    def _(k):
        g_copy(k).start()

    loads[4].wait()
    tile = min(512, cols)

    def y_copy(k):
        src = lax.rem(me + n - k, n)
        to = src // gc
        j = lax.rem(to + n_kv - kv, n_kv)
        pos = lax.rem(src, gc)
        return j, pos, pltpu.make_async_remote_copy(
            src_ref=ysend.at[k],
            dst_ref=red.at[j, pos],
            send_sem=y_ss.at[k],
            recv_sem=y_rs.at[j * gc + pos],
            device_id={"kv": to},
            device_id_type=MESH,
        )

    @pl.loop(0, n)
    def _(k):
        @pl.when(k > 0)
        def _():
            g_copy(k).wait_recv()

        j, pos, copy = y_copy(k)

        @pl.loop(0, cols // tile)
        def _(t):
            at = pl.ds(pl.multiple_of(t * tile, 128), tile)
            y = jnp.dot(gath[k], wbuf[:, at], preferred_element_type=f32)

            @pl.when(j == 0)
            def _():
                own[pos, :, at] = y

            @pl.when(j > 0)
            def _():
                ysend[k, :, at] = y.astype(bf16)

        @pl.when(j > 0)
        def _():
            copy.start()

    @pl.loop(0, gc)
    def _(pos):
        total = own[pos]
        for j in range(1, n_kv):
            pltpu.make_async_remote_copy(
                src_ref=ysend.at[0],
                dst_ref=red.at[j, pos],
                send_sem=y_ss.at[0],
                recv_sem=y_rs.at[j * gc + pos],
                device_id={"kv": lax.rem(kv + j, n_kv)},
                device_id_type=MESH,
            ).wait_recv()
            total = total + red[j, pos].astype(f32)
        o_ref[pos] = total.astype(bf16)

    @pl.loop(1, n)
    def _(k):
        q_copy(k).wait_send()
        po_copy(k).wait_send()
        pl_copy(k).wait_send()
        g_copy(k).wait_send()

    @pl.loop(0, n)
    def _(k):
        j, pos, copy = y_copy(k)

        @pl.when(j > 0)
        def _():
            copy.wait_send()


def local(
    queries,
    routes,
    suffix_lengths,
    prefix_keys,
    prefix_values,
    suffix_keys,
    suffix_values,
    new_keys,
    new_values,
    out_weight,
):
    n = lax.axis_size("dp")
    n_kv = lax.axis_size("kv")
    cands, steps, query_width = queries.shape
    kv_width = prefix_keys.shape[2]
    plen = prefix_keys.shape[1]
    depth = suffix_keys.shape[1]
    cols = out_weight.shape[1]
    heads = query_width // HD
    rows = cands * steps
    gc = n // n_kv
    cap = max(2, 2 * cands // n)
    me = lax.axis_index("dp")
    away = lax.rem(routes[:, 0] - me + n, n)
    order = jnp.arange(cands, dtype=jnp.int32)
    earlier = (away[:, None] == away[None, :]) & (order[None, :] < order[:, None])
    slot = away * cap + jnp.sum(earlier.astype(jnp.int32), 1)
    places = jnp.arange(n * cap, dtype=jnp.int32)
    inverse = jnp.sum(jnp.where(slot[None, :] == places[:, None], order[None, :], 0), 1)
    bf16, f32 = jnp.bfloat16, jnp.float32
    smem = pl.BlockSpec(memory_space=pltpu.SMEM)
    vmem = pl.BlockSpec(memory_space=pltpu.VMEM)
    hbm = pl.BlockSpec(memory_space=pl.ANY)
    dma = pltpu.SemaphoreType.DMA
    out = pl.pallas_call(
        functools.partial(kernel, n, n_kv, cap),
        out_shape=jax.ShapeDtypeStruct((gc, rows, cols), bf16),
        in_specs=[smem] * 3 + [vmem] * 3 + [hbm] * 5,
        out_specs=vmem,
        scratch_shapes=[
            pltpu.VMEM((plen, kv_width), bf16),
            pltpu.VMEM((plen, kv_width), bf16),
            pltpu.VMEM((cands, depth, kv_width), bf16),
            pltpu.VMEM((cands, depth, kv_width), bf16),
            pltpu.VMEM((query_width, cols), bf16),
            pltpu.VMEM((n, cap, steps, heads, HD), bf16),
            pltpu.VMEM((n, cap, steps, heads, HD), bf16),
            pltpu.VMEM((cands, steps, heads, HD), f32),
            pltpu.VMEM((cands, steps, heads, HD), f32),
            pltpu.VMEM((n, cap, steps, heads, HD), bf16),
            pltpu.VMEM((n, cap, steps, HD), f32),
            pltpu.VMEM((n * cap, steps, heads, HD), bf16),
            pltpu.VMEM((n * cap, steps, HD), f32),
            pltpu.VMEM((rows * heads, HD), f32),
            pltpu.VMEM((n, rows, query_width), bf16),
            pltpu.VMEM((n, rows, cols), bf16),
            pltpu.VMEM((n_kv, gc, rows, cols), bf16),
            pltpu.VMEM((gc, rows, cols), f32),
            dma((5,)),
            dma((n,)),
            dma((n,)),
            dma((n,)),
            dma((n,)),
            dma((n,)),
            dma((n,)),
            dma((n,)),
            dma((n,)),
            dma((n,)),
            dma((n_kv * gc,)),
        ],
        compiler_params=pltpu.CompilerParams(
            collective_id=0, has_side_effects=True, vmem_limit_bytes=60 * 1024 * 1024
        ),
    )(
        slot,
        inverse,
        suffix_lengths,
        queries.reshape(cands, steps, heads, HD),
        new_keys,
        new_values,
        prefix_keys[0],
        prefix_values[0],
        suffix_keys,
        suffix_values,
        out_weight,
    )
    return out.reshape(gc * cands, steps, cols)


def solution(mesh):
    placed = (
        P(("groups", "dp"), None, "kv"),
        P(("groups", "dp"), None),
        P(("groups", "dp")),
        P(("groups", "dp"), None, "kv"),
        P(("groups", "dp"), None, "kv"),
        P(("groups", "dp"), None, "kv"),
        P(("groups", "dp"), None, "kv"),
        P(("groups", "dp"), None, "kv"),
        P(("groups", "dp"), None, "kv"),
        P("kv", "dp"),
    )
    return jax.shard_map(
        local,
        mesh=mesh,
        in_specs=placed,
        out_specs=P(("groups", "kv"), None, "dp"),
        check_vma=False,
    )
```

```python
import functools
import math

import jax
import jax.numpy as jnp
from jax import lax
from jax.experimental import pallas as pl
from jax.experimental.pallas import tpu as pltpu
from jax.sharding import PartitionSpec as P

HD = 128
MESH = pl.DeviceIdType.MESH
NEG = -1e30


def kernel(
    n,
    n_kv,
    cap,
    route_ref,
    len_ref,
    q_ref,
    nk_ref,
    nv_ref,
    pk_hbm,
    pv_hbm,
    sk_hbm,
    sv_hbm,
    w_hbm,
    o_ref,
    kbuf,
    vbuf,
    skbuf,
    svbuf,
    wbuf,
    nkf,
    nvf,
    qx,
    sx,
    sl,
    qsend,
    qrecv,
    psend_o,
    psend_l,
    precv_o,
    precv_l,
    gath,
    ysend,
    red,
    own,
    local_sem,
    q_ss,
    q_rs,
    po_ss,
    po_rs,
    pl_ss,
    pl_rs,
    g_ss,
    g_rs,
    y_ss,
    y_rs,
):
    f32, bf16, i32 = jnp.float32, jnp.bfloat16, jnp.int32
    me = lax.axis_index("dp")
    kv = lax.axis_index("kv")
    rows, width = q_ref.shape
    cands = skbuf.shape[0]
    steps = rows // cands
    heads = width // HD
    kv_heads = kbuf.shape[1] // HD
    group = heads // kv_heads
    gw = group * HD
    pad = nkf.shape[0] // rows
    slots = qsend.shape[2]
    gc = n // n_kv
    cols = wbuf.shape[1]
    scale = 1.0 / math.sqrt(HD)

    loads = [
        pltpu.make_async_copy(src, dst, local_sem.at[i])
        for i, (src, dst) in enumerate(
            [(pk_hbm, kbuf), (pv_hbm, vbuf), (sk_hbm, skbuf), (sv_hbm, svbuf), (w_hbm, wbuf)]
        )
    ]
    for load in loads:
        load.start()

    barrier = pltpu.get_barrier_semaphore()

    @pl.loop(1, n)
    def _(k):
        pl.semaphore_signal(
            barrier, inc=1, device_id={"dp": lax.rem(me + k, n)}, device_id_type=MESH
        )

    @pl.loop(1, n_kv)
    def _(k):
        pl.semaphore_signal(
            barrier, inc=1, device_id={"kv": lax.rem(kv + k, n_kv)}, device_id_type=MESH
        )

    def tables():
        lane = lax.broadcasted_iota(i32, (cands, rows), 1)
        sub = lax.broadcasted_iota(i32, (cands, rows), 0)
        step = jnp.zeros((cands, rows), i32)
        for t in range(1, steps):
            step = step + jnp.where(lane >= t * cands, 1, 0)
        cand = lane - step * cands
        across = jnp.zeros((cands, rows), i32)
        down = jnp.zeros((cands, rows), i32)
        for c in range(cands):
            away = route_ref[c] - me
            away = jnp.where(away < 0, away + n, away)
            across = jnp.where(cand == c, away, across)
            down = jnp.where(sub == c, away, down)
        earlier = jnp.where((across == down) & (sub < cand), 1.0, 0.0)
        rank = jnp.sum(earlier, 0, keepdims=True)
        place = (across * slots + step * cap).astype(f32)[0:1] + rank
        pick = lax.broadcasted_iota(i32, (n * slots, rows), 0).astype(f32) == place
        eye = lax.broadcasted_iota(i32, (rows, rows), 0) == lax.broadcasted_iota(
            i32, (rows, rows), 1
        )
        column = jnp.sum(jnp.where(eye, place, 0.0), 1, keepdims=True)
        back = lax.broadcasted_iota(i32, (rows, n * slots), 1).astype(f32) == column
        return jnp.where(pick, 1.0, 0.0).astype(bf16), jnp.where(back, 1.0, 0.0)

    pick, back = tables()

    def dispatch(h):
        out = jnp.dot(pick, q_ref[:, h * gw : (h + 1) * gw], preferred_element_type=f32)
        for k in range(n):
            part = out[k * slots : (k + 1) * slots].astype(bf16)
            if k == 0:
                qrecv[h, 0] = part
            else:
                qsend[h, k] = part

    def turn(i):
        return 1 + lax.rem(i + n // 2 - 1, n - 1)

    def q_copy(h, k):
        return pltpu.make_async_remote_copy(
            src_ref=qsend.at[h, k],
            dst_ref=qrecv.at[h, k],
            send_sem=q_ss.at[h, k],
            recv_sem=q_rs.at[h, k],
            device_id={"dp": lax.rem(me + k, n)},
            device_id_type=MESH,
        )

    def po_copy(h, k):
        return pltpu.make_async_remote_copy(
            src_ref=psend_o.at[h, k],
            dst_ref=precv_o.at[h, k],
            send_sem=po_ss.at[h, k],
            recv_sem=po_rs.at[h, k],
            device_id={"dp": lax.rem(me + n - k, n)},
            device_id_type=MESH,
        )

    def pl_copy(h, k):
        return pltpu.make_async_remote_copy(
            src_ref=psend_l.at[h, k],
            dst_ref=precv_l.at[h, k],
            send_sem=pl_ss.at[h, k],
            recv_sem=pl_rs.at[h, k],
            device_id={"dp": lax.rem(me + n - k, n)},
            device_id_type=MESH,
        )

    def g_copy(side, h, src):
        to = me + 1 if side == 0 else me - 1
        return pltpu.make_async_remote_copy(
            src_ref=gath.at[h, src],
            dst_ref=gath.at[h, src],
            send_sem=g_ss.at[side, h, src],
            recv_sem=g_rs.at[h, src],
            device_id={"dp": lax.rem(to + n, n)},
            device_id_type=MESH,
        )

    for h in range(kv_heads):
        dispatch(h)
        if h == 0:
            pl.semaphore_wait(barrier, n - 1 + n_kv - 1)

        @pl.loop(0, n - 1)
        def _(i):
            q_copy(h, turn(i)).start()

    for hg in range(heads):
        qx[pl.ds(hg, rows, stride=heads), :] = q_ref[:, hg * HD : (hg + 1) * HD].astype(f32)
    for h in range(kv_heads):
        nkf[pl.ds(h, rows, stride=pad), :] = nk_ref[:, h * HD : (h + 1) * HD].astype(f32)
        nvf[pl.ds(h, rows, stride=pad), :] = nv_ref[:, h * HD : (h + 1) * HD].astype(f32)

    lane = lax.broadcasted_iota(i32, (slots, HD), 1)

    def attend(h, k):
        x = qrecv[h, k].astype(f32)
        x = jnp.concatenate([x[:, g * HD : (g + 1) * HD] for g in range(group)], 0)
        lanes = slice(h * HD, (h + 1) * HD)
        s = (
            lax.dot_general(
                x.astype(bf16),
                kbuf[:, lanes],
                (((1,), (1,)), ((), ())),
                preferred_element_type=f32,
            )
            * scale
        )
        top = jnp.max(s, 1, keepdims=True)
        p = jnp.exp(s - top)
        total = jnp.sum(p, 1, keepdims=True)
        o = jnp.dot(p.astype(bf16), vbuf[:, lanes], preferred_element_type=f32) / total
        lse = jnp.broadcast_to(top + jnp.log(total), (slots * group, HD))
        packed = jnp.zeros((slots, HD), f32)
        for g in range(group):
            packed = jnp.where(lane == g, lse[g * slots : (g + 1) * slots], packed)
        o = jnp.concatenate([o[g * slots : (g + 1) * slots] for g in range(group)], 1)
        return o.astype(bf16), packed

    depth = skbuf.shape[1]
    position = lax.broadcasted_iota(i32, (steps * group, depth), 1)
    row_of = lax.broadcasted_iota(i32, (steps * group, 1), 0)

    def suffix(c):
        length = len_ref[c]
        news_at = [
            pl.ds(pl.multiple_of((t * cands + c) * pad, 8), pad) for t in range(steps)
        ]
        for h in range(kv_heads):
            lanes = slice(h * HD, (h + 1) * HD)
            places = [
                pl.ds(pl.multiple_of((t * cands + c) * heads + h * group, 8), group)
                for t in range(steps)
            ]
            qh = jnp.concatenate([qx[place, :] for place in places], 0)
            s = lax.dot_general(
                qh.astype(bf16),
                skbuf[c, :, lanes],
                (((1,), (1,)), ((), ())),
                preferred_element_type=f32,
            )
            s = jnp.where(position < length, s * scale, NEG)
            top = jnp.max(s, 1, keepdims=True)
            news = []
            for t in range(steps):
                fresh = nkf[news_at[t], :][h : h + 1]
                f = jnp.sum(qh * fresh, 1, keepdims=True) * scale
                f = jnp.where(row_of >= t * group, f, NEG)
                top = jnp.maximum(top, f)
                news.append(f)
            p = jnp.exp(s - top)
            total = jnp.sum(p, 1, keepdims=True)
            o = jnp.dot(p.astype(bf16), svbuf[c, :, lanes], preferred_element_type=f32)
            for t in range(steps):
                e = jnp.exp(news[t] - top)
                total = total + e
                o = o + e * nvf[news_at[t], :][h : h + 1]
            o = o / total
            lse = jnp.broadcast_to(top + jnp.log(total), (steps * group, HD))
            for t, place in enumerate(places):
                sx[place, :] = o[t * group : (t + 1) * group]
                sl[place, :] = lse[t * group : (t + 1) * group]

    together = 4 if cands % 8 == 0 else 1
    half = cands // together // 2

    loads[0].wait()
    loads[1].wait()
    for h in range(kv_heads):
        o, packed = attend(h, 0)
        precv_o[h, 0] = o
        precv_l[h, 0] = packed
    loads[2].wait()
    loads[3].wait()

    @pl.loop(0, half)
    def _(i):
        for u in range(together):
            suffix(i * together + u)

    for h in range(kv_heads):

        @pl.loop(0, n - 1)
        def _(i):
            k = turn(i)
            q_copy(h, k).wait_recv()
            o, packed = attend(h, k)
            psend_o[h, k] = o
            psend_l[h, k] = packed
            po_copy(h, k).start()
            pl_copy(h, k).start()

    @pl.loop(half, cands // together)
    def _(i):
        for u in range(together):
            suffix(i * together + u)

    for h in range(kv_heads):

        @pl.loop(1, n)
        def _(k):
            po_copy(h, k).wait_recv()
            pl_copy(h, k).wait_recv()

        prompt = precv_o[h].astype(f32).reshape(n * slots, gw).astype(bf16)
        prompt = jnp.dot(back.astype(bf16), prompt, preferred_element_type=f32)
        totals = jnp.dot(
            back,
            precv_l[h].reshape(n * slots, HD),
            preferred_element_type=f32,
            precision=lax.Precision.HIGHEST,
        )
        for g in range(group):
            spot = pl.ds(h * group + g, rows, stride=heads)
            pt = totals[:, g : g + 1]
            st = sl[spot, :]
            peak = jnp.maximum(pt, st)
            a = jnp.exp(pt - peak)
            b = jnp.exp(st - peak)
            merged = (a * prompt[:, g * HD : (g + 1) * HD] + b * sx[spot, :]) / (a + b)
            gath[h, me, :, g * HD : (g + 1) * HD] = merged.astype(bf16)

        @pl.when(me < n - 1)
        def _():
            g_copy(0, h, me).start()

        @pl.when(me > 0)
        def _():
            g_copy(1, h, me).start()

    loads[4].wait()
    tile = min(512, cols)

    def y_copy(src):
        to = src // gc
        j = lax.rem(to + n_kv - kv, n_kv)
        pos = lax.rem(src, gc)
        return j, pos, pltpu.make_async_remote_copy(
            src_ref=ysend.at[src],
            dst_ref=red.at[j, pos],
            send_sem=y_ss.at[src],
            recv_sem=y_rs.at[j, pos],
            device_id={"kv": to},
            device_id_type=MESH,
        )

    def project(src):
        j, pos, copy = y_copy(src)

        @pl.loop(0, cols // tile)
        def _(t):
            at = pl.ds(pl.multiple_of(t * tile, 128), tile)
            y = jnp.dot(gath[0, src], wbuf[0:gw, at], preferred_element_type=f32)
            for h in range(1, kv_heads):
                y = y + jnp.dot(
                    gath[h, src], wbuf[h * gw : (h + 1) * gw, at], preferred_element_type=f32
                )

            @pl.when(j == 0)
            def _():
                own[pos, :, at] = y

            @pl.when(j > 0)
            def _():
                ysend[src, :, at] = y.astype(bf16)

        @pl.when(j > 0)
        def _():
            copy.start()

    project(me)

    @pl.loop(1, n)
    def _(d):
        before, after = me - d, me + d
        for h in range(kv_heads):

            @pl.when(before >= 0)
            def _():
                g_copy(0, h, before).wait_recv()

                @pl.when(me < n - 1)
                def _():
                    g_copy(0, h, before).start()

            @pl.when(after < n)
            def _():
                g_copy(1, h, after).wait_recv()

                @pl.when(me > 0)
                def _():
                    g_copy(1, h, after).start()

        @pl.loop(0, 2)
        def _(side):
            src = jnp.where(side == 0, before, after)

            @pl.when((src >= 0) & (src < n))
            def _():
                project(src)

    @pl.loop(0, gc)
    def _(pos):
        total = own[pos]
        for j in range(1, n_kv):
            pltpu.make_async_remote_copy(
                src_ref=ysend.at[0],
                dst_ref=red.at[j, pos],
                send_sem=y_ss.at[0],
                recv_sem=y_rs.at[j, pos],
                device_id={"kv": lax.rem(kv + j, n_kv)},
                device_id_type=MESH,
            ).wait_recv()
            total = total + red[j, pos].astype(f32)
        o_ref[pos] = total.astype(bf16)

    for h in range(kv_heads):

        @pl.loop(1, n)
        def _(k):
            q_copy(h, k).wait_send()
            po_copy(h, k).wait_send()
            pl_copy(h, k).wait_send()

        @pl.loop(0, n)
        def _(src):
            @pl.when((src <= me) & (me < n - 1))
            def _():
                g_copy(0, h, src).wait_send()

            @pl.when((src >= me) & (me > 0))
            def _():
                g_copy(1, h, src).wait_send()

    @pl.loop(0, n)
    def _(src):
        j, pos, copy = y_copy(src)

        @pl.when(j > 0)
        def _():
            copy.wait_send()


def local(
    queries,
    routes,
    suffix_lengths,
    prefix_keys,
    prefix_values,
    suffix_keys,
    suffix_values,
    new_keys,
    new_values,
    out_weight,
):
    n = lax.axis_size("dp")
    n_kv = lax.axis_size("kv")
    cands, steps, query_width = queries.shape
    kv_width = prefix_keys.shape[2]
    plen = prefix_keys.shape[1]
    depth = suffix_keys.shape[1]
    cols = out_weight.shape[1]
    heads = query_width // HD
    kv_heads = kv_width // HD
    gw = query_width // kv_heads
    rows = cands * steps
    gc = n // n_kv
    cap = max(2, 2 * cands // n)
    slots = -(-cap * steps // 8) * 8
    pad = -(-kv_heads // 8) * 8
    bf16, f32 = jnp.bfloat16, jnp.float32
    smem = pl.BlockSpec(memory_space=pltpu.SMEM)
    vmem = pl.BlockSpec(memory_space=pltpu.VMEM)
    hbm = pl.BlockSpec(memory_space=pl.ANY)
    dma = pltpu.SemaphoreType.DMA

    def by_step(x):
        return jnp.transpose(x, (1, 0, 2)).reshape(rows, x.shape[2])

    out = pl.pallas_call(
        functools.partial(kernel, n, n_kv, cap),
        out_shape=jax.ShapeDtypeStruct((gc, rows, cols), bf16),
        in_specs=[smem] * 2 + [vmem] * 3 + [hbm] * 5,
        out_specs=vmem,
        scratch_shapes=[
            pltpu.VMEM((plen, kv_width), bf16),
            pltpu.VMEM((plen, kv_width), bf16),
            pltpu.VMEM((cands, depth, kv_width), bf16),
            pltpu.VMEM((cands, depth, kv_width), bf16),
            pltpu.VMEM((query_width, cols), bf16),
            pltpu.VMEM((rows * pad, HD), f32),
            pltpu.VMEM((rows * pad, HD), f32),
            pltpu.VMEM((rows * heads, HD), f32),
            pltpu.VMEM((rows * heads, HD), f32),
            pltpu.VMEM((rows * heads, HD), f32),
            pltpu.VMEM((kv_heads, n, slots, gw), bf16),
            pltpu.VMEM((kv_heads, n, slots, gw), bf16),
            pltpu.VMEM((kv_heads, n, slots, gw), bf16),
            pltpu.VMEM((kv_heads, n, slots, HD), f32),
            pltpu.VMEM((kv_heads, n, slots, gw), bf16),
            pltpu.VMEM((kv_heads, n, slots, HD), f32),
            pltpu.VMEM((kv_heads, n, rows, gw), bf16),
            pltpu.VMEM((n, rows, cols), bf16),
            pltpu.VMEM((n_kv, gc, rows, cols), bf16),
            pltpu.VMEM((gc, rows, cols), f32),
            dma((5,)),
            dma((kv_heads, n)),
            dma((kv_heads, n)),
            dma((kv_heads, n)),
            dma((kv_heads, n)),
            dma((kv_heads, n)),
            dma((kv_heads, n)),
            dma((2, kv_heads, n)),
            dma((kv_heads, n)),
            dma((n,)),
            dma((n_kv, gc)),
        ],
        compiler_params=pltpu.CompilerParams(
            collective_id=0, has_side_effects=True, vmem_limit_bytes=60 * 1024 * 1024
        ),
    )(
        routes.reshape(cands),
        suffix_lengths,
        by_step(queries),
        by_step(new_keys),
        by_step(new_values),
        prefix_keys[0],
        prefix_values[0],
        suffix_keys,
        suffix_values,
        out_weight,
    )
    out = jnp.transpose(out.reshape(gc, steps, cands, cols), (0, 2, 1, 3))
    return out.reshape(gc * cands, steps, cols)


def solution(mesh):
    placed = (
        P(("groups", "dp"), None, "kv"),
        P(("groups", "dp"), None),
        P(("groups", "dp")),
        P(("groups", "dp"), None, "kv"),
        P(("groups", "dp"), None, "kv"),
        P(("groups", "dp"), None, "kv"),
        P(("groups", "dp"), None, "kv"),
        P(("groups", "dp"), None, "kv"),
        P(("groups", "dp"), None, "kv"),
        P("kv", "dp"),
    )
    return jax.shard_map(
        local,
        mesh=mesh,
        in_specs=placed,
        out_specs=P(("groups", "kv"), None, "dp"),
        check_vma=False,
    )
```

```python
import functools
import math

import jax
import jax.numpy as jnp
from jax import lax
from jax.experimental import pallas as pl
from jax.experimental.pallas import tpu as pltpu
from jax.sharding import PartitionSpec as P

HD = 128
MESH = pl.DeviceIdType.MESH
NEG = -1e30


def kernel(
    n,
    n_kv,
    cap,
    route_ref,
    len_ref,
    q_ref,
    nk_ref,
    nv_ref,
    pk_hbm,
    pv_hbm,
    sk_hbm,
    sv_hbm,
    w_hbm,
    o_ref,
    kbuf,
    vbuf,
    skbuf,
    svbuf,
    wbuf,
    nkf,
    nvf,
    qx,
    sx,
    sl,
    qsend,
    qrecv,
    psend_o,
    psend_l,
    precv_o,
    precv_l,
    gath,
    ysend,
    red,
    own,
    local_sem,
    q_ss,
    q_rs,
    po_ss,
    po_rs,
    pl_ss,
    pl_rs,
    g_ss,
    g_rs,
    y_ss,
    y_rs,
):
    f32, bf16, i32 = jnp.float32, jnp.bfloat16, jnp.int32
    me = lax.axis_index("dp")
    kv = lax.axis_index("kv")
    rows, width = q_ref.shape
    cands = skbuf.shape[0]
    steps = rows // cands
    heads = width // HD
    kv_heads = kbuf.shape[1] // HD
    group = heads // kv_heads
    gw = group * HD
    pad = nkf.shape[0] // rows
    slots = qsend.shape[2]
    gc = n // n_kv
    cols = wbuf.shape[1]
    scale = 1.0 / math.sqrt(HD)

    loads = [
        pltpu.make_async_copy(src, dst, local_sem.at[i])
        for i, (src, dst) in enumerate(
            [(pk_hbm, kbuf), (pv_hbm, vbuf), (sk_hbm, skbuf), (sv_hbm, svbuf), (w_hbm, wbuf)]
        )
    ]
    for load in loads:
        load.start()

    barrier = pltpu.get_barrier_semaphore()

    @pl.loop(1, n)
    def _(k):
        pl.semaphore_signal(
            barrier, inc=1, device_id={"dp": lax.rem(me + k, n)}, device_id_type=MESH
        )

    @pl.loop(1, n_kv)
    def _(k):
        pl.semaphore_signal(
            barrier, inc=1, device_id={"kv": lax.rem(kv + k, n_kv)}, device_id_type=MESH
        )

    def tables():
        lane = lax.broadcasted_iota(i32, (cands, rows), 1)
        sub = lax.broadcasted_iota(i32, (cands, rows), 0)
        step = jnp.zeros((cands, rows), i32)
        for t in range(1, steps):
            step = step + jnp.where(lane >= t * cands, 1, 0)
        cand = lane - step * cands
        across = jnp.zeros((cands, rows), i32)
        down = jnp.zeros((cands, rows), i32)
        for c in range(cands):
            away = route_ref[c] - me
            away = jnp.where(away < 0, away + n, away)
            across = jnp.where(cand == c, away, across)
            down = jnp.where(sub == c, away, down)
        earlier = jnp.where((across == down) & (sub < cand), 1.0, 0.0)
        rank = jnp.sum(earlier, 0, keepdims=True)
        place = (across * slots + step * cap).astype(f32)[0:1] + rank
        pick = lax.broadcasted_iota(i32, (n * slots, rows), 0).astype(f32) == place
        eye = lax.broadcasted_iota(i32, (rows, rows), 0) == lax.broadcasted_iota(
            i32, (rows, rows), 1
        )
        column = jnp.sum(jnp.where(eye, place, 0.0), 1, keepdims=True)
        back = lax.broadcasted_iota(i32, (rows, n * slots), 1).astype(f32) == column
        return jnp.where(pick, 1.0, 0.0).astype(bf16), jnp.where(back, 1.0, 0.0)

    pick, back = tables()

    def dispatch(h):
        out = jnp.dot(pick, q_ref[:, h * gw : (h + 1) * gw], preferred_element_type=f32)
        for k in range(n):
            part = out[k * slots : (k + 1) * slots].astype(bf16)
            if k == 0:
                qrecv[h, 0] = part
            else:
                qsend[h, k] = part

    def turn(i):
        return 1 + lax.rem(i + n // 2 - 1, n - 1)

    def q_copy(h, k):
        return pltpu.make_async_remote_copy(
            src_ref=qsend.at[h, k],
            dst_ref=qrecv.at[h, k],
            send_sem=q_ss.at[h, k],
            recv_sem=q_rs.at[h, k],
            device_id={"dp": lax.rem(me + k, n)},
            device_id_type=MESH,
        )

    def po_copy(h, k):
        return pltpu.make_async_remote_copy(
            src_ref=psend_o.at[h, k],
            dst_ref=precv_o.at[h, k],
            send_sem=po_ss.at[h, k],
            recv_sem=po_rs.at[h, k],
            device_id={"dp": lax.rem(me + n - k, n)},
            device_id_type=MESH,
        )

    def pl_copy(h, k):
        return pltpu.make_async_remote_copy(
            src_ref=psend_l.at[h, k],
            dst_ref=precv_l.at[h, k],
            send_sem=pl_ss.at[h, k],
            recv_sem=pl_rs.at[h, k],
            device_id={"dp": lax.rem(me + n - k, n)},
            device_id_type=MESH,
        )

    def g_copy(side, h, src):
        to = me + 1 if side == 0 else me - 1
        return pltpu.make_async_remote_copy(
            src_ref=gath.at[h, src],
            dst_ref=gath.at[h, src],
            send_sem=g_ss.at[side, h, src],
            recv_sem=g_rs.at[h, src],
            device_id={"dp": lax.rem(to + n, n)},
            device_id_type=MESH,
        )

    def ask(h):
        @pl.loop(0, n - 1)
        def _(i):
            q_copy(h, turn(i)).start()

    dispatch(0)
    pl.semaphore_wait(barrier, n - 1 + n_kv - 1)
    ask(0)
    for h in range(1, kv_heads):
        dispatch(h)

    for hg in range(heads):
        qx[pl.ds(hg, rows, stride=heads), :] = q_ref[:, hg * HD : (hg + 1) * HD].astype(f32)
    for h in range(kv_heads):
        nkf[pl.ds(h, rows, stride=pad), :] = nk_ref[:, h * HD : (h + 1) * HD].astype(f32)
        nvf[pl.ds(h, rows, stride=pad), :] = nv_ref[:, h * HD : (h + 1) * HD].astype(f32)

    tiles = slots // 8
    lane = lax.broadcasted_iota(i32, (8, HD), 1)

    def attend(h, k):
        x = qrecv[h, k].astype(f32)
        x = jnp.concatenate([x[:, g * HD : (g + 1) * HD] for g in range(group)], 0)
        lanes = slice(h * HD, (h + 1) * HD)
        s = (
            lax.dot_general(
                x.astype(bf16),
                kbuf[:, lanes],
                (((1,), (1,)), ((), ())),
                preferred_element_type=f32,
            )
            * scale
        )
        top = jnp.max(s, 1, keepdims=True)
        p = jnp.exp(s - top)
        total = jnp.sum(p, 1, keepdims=True)
        o = jnp.dot(p.astype(bf16), vbuf[:, lanes], preferred_element_type=f32) / total
        lse = jnp.broadcast_to(top + jnp.log(total), (slots * group, HD))
        packed = jnp.zeros((8, HD), f32)
        for g in range(group):
            for t in range(tiles):
                at = g * slots + t * 8
                packed = jnp.where(lane == t * group + g, lse[at : at + 8], packed)
        o = jnp.concatenate([o[g * slots : (g + 1) * slots] for g in range(group)], 1)
        return o.astype(bf16), packed

    depth = skbuf.shape[1]
    position = lax.broadcasted_iota(i32, (steps * group, depth), 1)
    row_of = lax.broadcasted_iota(i32, (steps * group, 1), 0)

    def suffix(h, c):
        length = len_ref[c]
        news_at = [
            pl.ds(pl.multiple_of((t * cands + c) * pad, 8), pad) for t in range(steps)
        ]
        lanes = slice(h * HD, (h + 1) * HD)
        places = [
            pl.ds(pl.multiple_of((t * cands + c) * heads + h * group, 8), group)
            for t in range(steps)
        ]
        qh = jnp.concatenate([qx[place, :] for place in places], 0)
        s = lax.dot_general(
            qh.astype(bf16),
            skbuf[c, :, lanes],
            (((1,), (1,)), ((), ())),
            preferred_element_type=f32,
        )
        s = jnp.where(position < length, s * scale, NEG)
        top = jnp.max(s, 1, keepdims=True)
        news = []
        for t in range(steps):
            fresh = nkf[news_at[t], :][h : h + 1]
            f = jnp.sum(qh * fresh, 1, keepdims=True) * scale
            f = jnp.where(row_of >= t * group, f, NEG)
            top = jnp.maximum(top, f)
            news.append(f)
        p = jnp.exp(s - top)
        total = jnp.sum(p, 1, keepdims=True)
        o = jnp.dot(p.astype(bf16), svbuf[c, :, lanes], preferred_element_type=f32)
        for t in range(steps):
            e = jnp.exp(news[t] - top)
            total = total + e
            o = o + e * nvf[news_at[t], :][h : h + 1]
        o = o / total
        lse = jnp.broadcast_to(top + jnp.log(total), (steps * group, HD))
        for t, place in enumerate(places):
            sx[place, :] = o[t * group : (t + 1) * group]
            sl[place, :] = lse[t * group : (t + 1) * group]

    together = 8 if cands % 8 == 0 else 1

    def suffixes(h):
        @pl.loop(0, cands // together)
        def _(i):
            for u in range(together):
                suffix(h, i * together + u)

    def here(h):
        o, packed = attend(h, 0)
        precv_o[h, 0] = o
        precv_l[h, 0] = packed

    def serve(h):
        @pl.loop(0, n - 1)
        def _(i):
            k = turn(i)
            q_copy(h, k).wait_recv()
            o, packed = attend(h, k)
            psend_o[h, k] = o
            psend_l[h, k] = packed
            pl_copy(h, k).start()
            po_copy(h, k).start()

    def merge(h):
        @pl.loop(1, n)
        def _(k):
            po_copy(h, k).wait_recv()
            pl_copy(h, k).wait_recv()

        prompt = precv_o[h].astype(f32).reshape(n * slots, gw).astype(bf16)
        prompt = jnp.dot(back.astype(bf16), prompt, preferred_element_type=f32)
        wide = lax.broadcasted_iota(i32, (n, 8, HD), 2)
        packed = precv_l[h]
        spread = jnp.concatenate(
            [
                jnp.where((wide >= t * group) & (wide < (t + 1) * group), packed, 0.0)[:, None]
                for t in range(tiles)
            ],
            1,
        ).reshape(n * slots, HD)
        totals = jnp.dot(
            back,
            spread,
            preferred_element_type=f32,
            precision=lax.Precision.HIGHEST,
        )
        for g in range(group):
            spot = pl.ds(h * group + g, rows, stride=heads)
            pt = totals[:, g : g + 1]
            for t in range(1, tiles):
                pt = pt + totals[:, t * group + g : t * group + g + 1]
            st = sl[spot, :]
            peak = jnp.maximum(pt, st)
            a = jnp.exp(pt - peak)
            b = jnp.exp(st - peak)
            merged = (a * prompt[:, g * HD : (g + 1) * HD] + b * sx[spot, :]) / (a + b)
            gath[h, me, :, g * HD : (g + 1) * HD] = merged.astype(bf16)

        @pl.when(me < n - 1)
        def _():
            g_copy(0, h, me).start()

        @pl.when(me > 0)
        def _():
            g_copy(1, h, me).start()

    def relay(h, d):
        before, after = me - d, me + d

        @pl.when(before >= 0)
        def _():
            g_copy(0, h, before).wait_recv()

            @pl.when(me < n - 1)
            def _():
                g_copy(0, h, before).start()

        @pl.when(after < n)
        def _():
            g_copy(1, h, after).wait_recv()

            @pl.when(me > 0)
            def _():
                g_copy(1, h, after).start()

    loads[0].wait()
    loads[1].wait()
    here(0)
    serve(0)
    for h in range(kv_heads):
        if h + 1 < kv_heads:
            ask(h + 1)
        if h == 0:
            loads[2].wait()
            loads[3].wait()
            suffixes(h)
        merge(h)
        if h + 1 < kv_heads:
            here(h + 1)
            suffixes(h + 1)
            relay(h, 1)
            serve(h + 1)

            @pl.loop(2, n)
            def _(d):
                relay(h, d)

    loads[4].wait()
    tile = min(512, cols)

    def y_copy(src, t):
        to = src // gc
        j = lax.rem(to + n_kv - kv, n_kv)
        pos = lax.rem(src, gc)
        at = pl.ds(pl.multiple_of(t * tile, 128), tile)
        return j, pos, pltpu.make_async_remote_copy(
            src_ref=ysend.at[src, :, at],
            dst_ref=red.at[j, pos, :, at],
            send_sem=y_ss.at[src, t],
            recv_sem=y_rs.at[j, pos, t],
            device_id={"kv": to},
            device_id_type=MESH,
        )

    def project(src):
        @pl.loop(0, cols // tile)
        def _(t):
            j, pos, copy = y_copy(src, t)
            at = pl.ds(pl.multiple_of(t * tile, 128), tile)
            y = jnp.dot(gath[0, src], wbuf[0:gw, at], preferred_element_type=f32)
            for h in range(1, kv_heads):
                y = y + jnp.dot(
                    gath[h, src], wbuf[h * gw : (h + 1) * gw, at], preferred_element_type=f32
                )

            @pl.when(j == 0)
            def _():
                own[pos, :, at] = y

            @pl.when(j > 0)
            def _():
                ysend[src, :, at] = y.astype(bf16)
                copy.start()

    project(me)

    @pl.loop(1, n)
    def _(d):
        relay(kv_heads - 1, d)

        @pl.loop(0, 2)
        def _(side):
            src = jnp.where(side == 0, me - d, me + d)

            @pl.when((src >= 0) & (src < n))
            def _():
                project(src)

    @pl.loop(0, gc)
    def _(pos):
        @pl.loop(0, cols // tile)
        def _(t):
            at = pl.ds(pl.multiple_of(t * tile, 128), tile)
            total = own[pos, :, at]
            for j in range(1, n_kv):
                pltpu.make_async_remote_copy(
                    src_ref=ysend.at[0, :, at],
                    dst_ref=red.at[j, pos, :, at],
                    send_sem=y_ss.at[0, t],
                    recv_sem=y_rs.at[j, pos, t],
                    device_id={"kv": lax.rem(kv + j, n_kv)},
                    device_id_type=MESH,
                ).wait_recv()
                total = total + red[j, pos, :, at].astype(f32)
            o_ref[pos, :, at] = total.astype(bf16)

    for h in range(kv_heads):

        @pl.loop(1, n)
        def _(k):
            q_copy(h, k).wait_send()
            po_copy(h, k).wait_send()
            pl_copy(h, k).wait_send()

        @pl.loop(0, n)
        def _(src):
            @pl.when((src <= me) & (me < n - 1))
            def _():
                g_copy(0, h, src).wait_send()

            @pl.when((src >= me) & (me > 0))
            def _():
                g_copy(1, h, src).wait_send()

    @pl.loop(0, n)
    def _(src):
        @pl.loop(0, cols // tile)
        def _(t):
            j, pos, copy = y_copy(src, t)

            @pl.when(j > 0)
            def _():
                copy.wait_send()


def local(
    queries,
    routes,
    suffix_lengths,
    prefix_keys,
    prefix_values,
    suffix_keys,
    suffix_values,
    new_keys,
    new_values,
    out_weight,
):
    n = lax.axis_size("dp")
    n_kv = lax.axis_size("kv")
    cands, steps, query_width = queries.shape
    kv_width = prefix_keys.shape[2]
    plen = prefix_keys.shape[1]
    depth = suffix_keys.shape[1]
    cols = out_weight.shape[1]
    heads = query_width // HD
    kv_heads = kv_width // HD
    gw = query_width // kv_heads
    rows = cands * steps
    gc = n // n_kv
    cap = max(2, 2 * cands // n)
    slots = -(-cap * steps // 8) * 8
    pad = -(-kv_heads // 8) * 8
    bf16, f32 = jnp.bfloat16, jnp.float32
    smem = pl.BlockSpec(memory_space=pltpu.SMEM)
    vmem = pl.BlockSpec(memory_space=pltpu.VMEM)
    hbm = pl.BlockSpec(memory_space=pl.ANY)
    dma = pltpu.SemaphoreType.DMA

    def by_step(x):
        return jnp.transpose(x, (1, 0, 2)).reshape(rows, x.shape[2])

    out = pl.pallas_call(
        functools.partial(kernel, n, n_kv, cap),
        out_shape=jax.ShapeDtypeStruct((gc, rows, cols), bf16),
        in_specs=[smem] * 2 + [vmem] * 3 + [hbm] * 5,
        out_specs=vmem,
        scratch_shapes=[
            pltpu.VMEM((plen, kv_width), bf16),
            pltpu.VMEM((plen, kv_width), bf16),
            pltpu.VMEM((cands, depth, kv_width), bf16),
            pltpu.VMEM((cands, depth, kv_width), bf16),
            pltpu.VMEM((query_width, cols), bf16),
            pltpu.VMEM((rows * pad, HD), f32),
            pltpu.VMEM((rows * pad, HD), f32),
            pltpu.VMEM((rows * heads, HD), f32),
            pltpu.VMEM((rows * heads, HD), f32),
            pltpu.VMEM((rows * heads, HD), f32),
            pltpu.VMEM((kv_heads, n, slots, gw), bf16),
            pltpu.VMEM((kv_heads, n, slots, gw), bf16),
            pltpu.VMEM((kv_heads, n, slots, gw), bf16),
            pltpu.VMEM((kv_heads, n, 8, HD), f32),
            pltpu.VMEM((kv_heads, n, slots, gw), bf16),
            pltpu.VMEM((kv_heads, n, 8, HD), f32),
            pltpu.VMEM((kv_heads, n, rows, gw), bf16),
            pltpu.VMEM((n, rows, cols), bf16),
            pltpu.VMEM((n_kv, gc, rows, cols), bf16),
            pltpu.VMEM((gc, rows, cols), f32),
            dma((5,)),
            dma((kv_heads, n)),
            dma((kv_heads, n)),
            dma((kv_heads, n)),
            dma((kv_heads, n)),
            dma((kv_heads, n)),
            dma((kv_heads, n)),
            dma((2, kv_heads, n)),
            dma((kv_heads, n)),
            dma((n, cols // min(512, cols))),
            dma((n_kv, gc, cols // min(512, cols))),
        ],
        compiler_params=pltpu.CompilerParams(
            collective_id=0, has_side_effects=True, vmem_limit_bytes=60 * 1024 * 1024
        ),
    )(
        routes.reshape(cands),
        suffix_lengths,
        by_step(queries),
        by_step(new_keys),
        by_step(new_values),
        prefix_keys[0],
        prefix_values[0],
        suffix_keys,
        suffix_values,
        out_weight,
    )
    out = jnp.transpose(out.reshape(gc, steps, cands, cols), (0, 2, 1, 3))
    return out.reshape(gc * cands, steps, cols)


def solution(mesh):
    placed = (
        P(("groups", "dp"), None, "kv"),
        P(("groups", "dp"), None),
        P(("groups", "dp")),
        P(("groups", "dp"), None, "kv"),
        P(("groups", "dp"), None, "kv"),
        P(("groups", "dp"), None, "kv"),
        P(("groups", "dp"), None, "kv"),
        P(("groups", "dp"), None, "kv"),
        P(("groups", "dp"), None, "kv"),
        P("kv", "dp"),
    )
    return jax.shard_map(
        local,
        mesh=mesh,
        in_specs=placed,
        out_specs=P(("groups", "kv"), None, "dp"),
        check_vma=False,
    )
```

```python
import functools
import math

import jax
import jax.numpy as jnp
from jax import lax
from jax.experimental import pallas as pl
from jax.experimental.pallas import tpu as pltpu
from jax.sharding import PartitionSpec as P

HD = 128
MESH = pl.DeviceIdType.MESH
NEG = -1e30


def kernel(
    n,
    n_kv,
    cap,
    route_ref,
    len_ref,
    q_ref,
    nk_ref,
    nv_ref,
    pk_hbm,
    pv_hbm,
    sk_hbm,
    sv_hbm,
    w_hbm,
    o_ref,
    kbuf,
    vbuf,
    skbuf,
    svbuf,
    wbuf,
    nkf,
    nvf,
    qx,
    sx,
    sl,
    qsend,
    qrecv,
    psend_o,
    psend_l,
    precv_o,
    precv_l,
    gath,
    ysend,
    red,
    own,
    local_sem,
    q_ss,
    q_rs,
    po_ss,
    po_rs,
    pl_ss,
    pl_rs,
    g_ss,
    g_rs,
    y_ss,
    y_rs,
):
    f32, bf16, i32 = jnp.float32, jnp.bfloat16, jnp.int32
    me = lax.axis_index("dp")
    kv = lax.axis_index("kv")
    rows, width = q_ref.shape
    cands = skbuf.shape[0]
    steps = rows // cands
    heads = width // HD
    kv_heads = kbuf.shape[1] // HD
    group = heads // kv_heads
    gw = group * HD
    pad = nkf.shape[0] // rows
    slots = qsend.shape[2]
    gc = n // n_kv
    cols = wbuf.shape[1]
    scale = 1.0 / math.sqrt(HD)

    loads = [
        pltpu.make_async_copy(src, dst, local_sem.at[i])
        for i, (src, dst) in enumerate(
            [(pk_hbm, kbuf), (pv_hbm, vbuf), (sk_hbm, skbuf), (sv_hbm, svbuf), (w_hbm, wbuf)]
        )
    ]
    for load in loads:
        load.start()

    barrier = pltpu.get_barrier_semaphore()

    @pl.loop(1, n)
    def _(k):
        pl.semaphore_signal(
            barrier, inc=1, device_id={"dp": lax.rem(me + k, n)}, device_id_type=MESH
        )

    @pl.loop(1, n_kv)
    def _(k):
        pl.semaphore_signal(
            barrier, inc=1, device_id={"kv": lax.rem(kv + k, n_kv)}, device_id_type=MESH
        )

    def tables():
        lane = lax.broadcasted_iota(i32, (cands, rows), 1)
        sub = lax.broadcasted_iota(i32, (cands, rows), 0)
        step = jnp.zeros((cands, rows), i32)
        for t in range(1, steps):
            step = step + jnp.where(lane >= t * cands, 1, 0)
        cand = lane - step * cands
        across = jnp.zeros((cands, rows), i32)
        down = jnp.zeros((cands, rows), i32)
        for c in range(cands):
            away = route_ref[c] - me
            away = jnp.where(away < 0, away + n, away)
            across = jnp.where(cand == c, away, across)
            down = jnp.where(sub == c, away, down)
        earlier = jnp.where((across == down) & (sub < cand), 1.0, 0.0)
        rank = jnp.sum(earlier, 0, keepdims=True)
        place = (across * slots + step * cap).astype(f32)[0:1] + rank
        pick = lax.broadcasted_iota(i32, (n * slots, rows), 0).astype(f32) == place
        eye = lax.broadcasted_iota(i32, (rows, rows), 0) == lax.broadcasted_iota(
            i32, (rows, rows), 1
        )
        column = jnp.sum(jnp.where(eye, place, 0.0), 1, keepdims=True)
        back = lax.broadcasted_iota(i32, (rows, n * slots), 1).astype(f32) == column
        return jnp.where(pick, 1.0, 0.0).astype(bf16), jnp.where(back, 1.0, 0.0)

    pick, back = tables()

    def dispatch(h):
        out = jnp.dot(pick, q_ref[:, h * gw : (h + 1) * gw], preferred_element_type=f32)
        for k in range(n):
            part = out[k * slots : (k + 1) * slots].astype(bf16)
            if k == 0:
                qrecv[h, 0] = part
            else:
                qsend[h, k] = part

    def turn(i):
        return 1 + i

    def q_copy(h, k):
        return pltpu.make_async_remote_copy(
            src_ref=qsend.at[h, k],
            dst_ref=qrecv.at[h, k],
            send_sem=q_ss.at[h, k],
            recv_sem=q_rs.at[h, k],
            device_id={"dp": lax.rem(me + k, n)},
            device_id_type=MESH,
        )

    def po_copy(h, k):
        return pltpu.make_async_remote_copy(
            src_ref=psend_o.at[h, k],
            dst_ref=precv_o.at[h, k],
            send_sem=po_ss.at[h, k],
            recv_sem=po_rs.at[h, k],
            device_id={"dp": lax.rem(me + n - k, n)},
            device_id_type=MESH,
        )

    def pl_copy(h, k):
        return pltpu.make_async_remote_copy(
            src_ref=psend_l.at[h, k],
            dst_ref=precv_l.at[h, k],
            send_sem=pl_ss.at[h, k],
            recv_sem=pl_rs.at[h, k],
            device_id={"dp": lax.rem(me + n - k, n)},
            device_id_type=MESH,
        )

    def g_copy(side, h, src):
        to = me + 1 if side == 0 else me - 1
        return pltpu.make_async_remote_copy(
            src_ref=gath.at[h, src],
            dst_ref=gath.at[h, src],
            send_sem=g_ss.at[side, h, src],
            recv_sem=g_rs.at[h, src],
            device_id={"dp": lax.rem(to + n, n)},
            device_id_type=MESH,
        )

    def ask(h):
        @pl.loop(0, n - 1)
        def _(i):
            q_copy(h, turn(i)).start()

    dispatch(0)
    pl.semaphore_wait(barrier, n - 1 + n_kv - 1)
    ask(0)
    for h in range(1, kv_heads):
        dispatch(h)
        ask(h)

    for hg in range(heads):
        qx[pl.ds(hg, rows, stride=heads), :] = q_ref[:, hg * HD : (hg + 1) * HD].astype(f32)
    for h in range(kv_heads):
        nkf[pl.ds(h, rows, stride=pad), :] = nk_ref[:, h * HD : (h + 1) * HD].astype(f32)
        nvf[pl.ds(h, rows, stride=pad), :] = nv_ref[:, h * HD : (h + 1) * HD].astype(f32)

    tiles = slots // 8
    lane = lax.broadcasted_iota(i32, (8, HD), 1)

    def attend(h, k):
        x = qrecv[h, k].astype(f32)
        x = jnp.concatenate([x[:, g * HD : (g + 1) * HD] for g in range(group)], 0)
        lanes = slice(h * HD, (h + 1) * HD)
        s = (
            lax.dot_general(
                x.astype(bf16),
                kbuf[:, lanes],
                (((1,), (1,)), ((), ())),
                preferred_element_type=f32,
            )
            * scale
        )
        top = jnp.max(s, 1, keepdims=True)
        p = jnp.exp(s - top)
        total = jnp.sum(p, 1, keepdims=True)
        o = jnp.dot(p.astype(bf16), vbuf[:, lanes], preferred_element_type=f32) / total
        lse = jnp.broadcast_to(top + jnp.log(total), (slots * group, HD))
        packed = jnp.zeros((8, HD), f32)
        for g in range(group):
            for t in range(tiles):
                at = g * slots + t * 8
                packed = jnp.where(lane == t * group + g, lse[at : at + 8], packed)
        o = jnp.concatenate([o[g * slots : (g + 1) * slots] for g in range(group)], 1)
        return o.astype(bf16), packed

    depth = skbuf.shape[1]
    position = lax.broadcasted_iota(i32, (steps * group, depth), 1)
    row_of = lax.broadcasted_iota(i32, (steps * group, 1), 0)

    def suffix(h, c):
        length = len_ref[c]
        news_at = [
            pl.ds(pl.multiple_of((t * cands + c) * pad, 8), pad) for t in range(steps)
        ]
        lanes = slice(h * HD, (h + 1) * HD)
        places = [
            pl.ds(pl.multiple_of((t * cands + c) * heads + h * group, 8), group)
            for t in range(steps)
        ]
        qh = jnp.concatenate([qx[place, :] for place in places], 0)
        s = lax.dot_general(
            qh.astype(bf16),
            skbuf[c, :, lanes],
            (((1,), (1,)), ((), ())),
            preferred_element_type=f32,
        )
        s = jnp.where(position < length, s * scale, NEG)
        top = jnp.max(s, 1, keepdims=True)
        news = []
        for t in range(steps):
            fresh = nkf[news_at[t], :][h : h + 1]
            f = jnp.sum(qh * fresh, 1, keepdims=True) * scale
            f = jnp.where(row_of >= t * group, f, NEG)
            top = jnp.maximum(top, f)
            news.append(f)
        p = jnp.exp(s - top)
        total = jnp.sum(p, 1, keepdims=True)
        o = jnp.dot(p.astype(bf16), svbuf[c, :, lanes], preferred_element_type=f32)
        for t in range(steps):
            e = jnp.exp(news[t] - top)
            total = total + e
            o = o + e * nvf[news_at[t], :][h : h + 1]
        o = o / total
        lse = jnp.broadcast_to(top + jnp.log(total), (steps * group, HD))
        for t, place in enumerate(places):
            sx[place, :] = o[t * group : (t + 1) * group]
            sl[place, :] = lse[t * group : (t + 1) * group]

    together = 8 if cands % 8 == 0 else 1

    def suffixes(h):
        @pl.loop(0, cands // together)
        def _(i):
            for u in range(together):
                suffix(h, i * together + u)

    def here(h):
        o, packed = attend(h, 0)
        precv_o[h, 0] = o
        precv_l[h, 0] = packed

    def serve(h):
        @pl.loop(0, n - 1)
        def _(i):
            k = turn(i)
            q_copy(h, k).wait_recv()
            o, packed = attend(h, k)
            psend_o[h, k] = o
            psend_l[h, k] = packed
            pl_copy(h, k).start()
            po_copy(h, k).start()

    def merge(h):
        @pl.loop(1, n)
        def _(k):
            po_copy(h, k).wait_recv()
            pl_copy(h, k).wait_recv()

        prompt = precv_o[h].astype(f32).reshape(n * slots, gw).astype(bf16)
        prompt = jnp.dot(back.astype(bf16), prompt, preferred_element_type=f32)
        wide = lax.broadcasted_iota(i32, (n, 8, HD), 2)
        packed = precv_l[h]
        spread = jnp.concatenate(
            [
                jnp.where((wide >= t * group) & (wide < (t + 1) * group), packed, 0.0)[:, None]
                for t in range(tiles)
            ],
            1,
        ).reshape(n * slots, HD)
        totals = jnp.dot(
            back,
            spread,
            preferred_element_type=f32,
            precision=lax.Precision.HIGHEST,
        )
        for g in range(group):
            spot = pl.ds(h * group + g, rows, stride=heads)
            pt = totals[:, g : g + 1]
            for t in range(1, tiles):
                pt = pt + totals[:, t * group + g : t * group + g + 1]
            st = sl[spot, :]
            peak = jnp.maximum(pt, st)
            a = jnp.exp(pt - peak)
            b = jnp.exp(st - peak)
            merged = (a * prompt[:, g * HD : (g + 1) * HD] + b * sx[spot, :]) / (a + b)
            gath[h, me, :, g * HD : (g + 1) * HD] = merged.astype(bf16)

        @pl.when(me < n - 1)
        def _():
            g_copy(0, h, me).start()

        @pl.when(me > 0)
        def _():
            g_copy(1, h, me).start()

    def relay(h, d):
        before, after = me - d, me + d

        @pl.when(before >= 0)
        def _():
            g_copy(0, h, before).wait_recv()

            @pl.when(me < n - 1)
            def _():
                g_copy(0, h, before).start()

        @pl.when(after < n)
        def _():
            g_copy(1, h, after).wait_recv()

            @pl.when(me > 0)
            def _():
                g_copy(1, h, after).start()

    loads[0].wait()
    loads[1].wait()
    for h in range(kv_heads):
        here(h)
    loads[2].wait()
    loads[3].wait()
    suffixes(0)
    for h in range(kv_heads):
        serve(h)
    for h in range(1, kv_heads):
        suffixes(h)
    for h in range(kv_heads):
        merge(h)

    loads[4].wait()
    tile = min(512, cols)

    def y_copy(src, t):
        to = src // gc
        j = lax.rem(to + n_kv - kv, n_kv)
        pos = lax.rem(src, gc)
        at = pl.ds(pl.multiple_of(t * tile, 128), tile)
        return j, pos, pltpu.make_async_remote_copy(
            src_ref=ysend.at[src, :, at],
            dst_ref=red.at[j, pos, :, at],
            send_sem=y_ss.at[src, t],
            recv_sem=y_rs.at[j, pos, t],
            device_id={"kv": to},
            device_id_type=MESH,
        )

    def project(src):
        @pl.loop(0, cols // tile)
        def _(t):
            j, pos, copy = y_copy(src, t)
            at = pl.ds(pl.multiple_of(t * tile, 128), tile)
            y = jnp.dot(gath[0, src], wbuf[0:gw, at], preferred_element_type=f32)
            for h in range(1, kv_heads):
                y = y + jnp.dot(
                    gath[h, src], wbuf[h * gw : (h + 1) * gw, at], preferred_element_type=f32
                )

            @pl.when(j == 0)
            def _():
                own[pos, :, at] = y

            @pl.when(j > 0)
            def _():
                ysend[src, :, at] = y.astype(bf16)
                copy.start()

    project(me)

    @pl.loop(1, n)
    def _(d):
        for h in range(kv_heads):
            relay(h, d)

        @pl.loop(0, 2)
        def _(side):
            src = jnp.where(side == 0, me - d, me + d)

            @pl.when((src >= 0) & (src < n))
            def _():
                project(src)

    @pl.loop(0, gc)
    def _(pos):
        @pl.loop(0, cols // tile)
        def _(t):
            at = pl.ds(pl.multiple_of(t * tile, 128), tile)
            total = own[pos, :, at]
            for j in range(1, n_kv):
                pltpu.make_async_remote_copy(
                    src_ref=ysend.at[0, :, at],
                    dst_ref=red.at[j, pos, :, at],
                    send_sem=y_ss.at[0, t],
                    recv_sem=y_rs.at[j, pos, t],
                    device_id={"kv": lax.rem(kv + j, n_kv)},
                    device_id_type=MESH,
                ).wait_recv()
                total = total + red[j, pos, :, at].astype(f32)
            o_ref[pos, :, at] = total.astype(bf16)

    for h in range(kv_heads):

        @pl.loop(1, n)
        def _(k):
            q_copy(h, k).wait_send()
            po_copy(h, k).wait_send()
            pl_copy(h, k).wait_send()

        @pl.loop(0, n)
        def _(src):
            @pl.when((src <= me) & (me < n - 1))
            def _():
                g_copy(0, h, src).wait_send()

            @pl.when((src >= me) & (me > 0))
            def _():
                g_copy(1, h, src).wait_send()

    @pl.loop(0, n)
    def _(src):
        @pl.loop(0, cols // tile)
        def _(t):
            j, pos, copy = y_copy(src, t)

            @pl.when(j > 0)
            def _():
                copy.wait_send()


def local(
    queries,
    routes,
    suffix_lengths,
    prefix_keys,
    prefix_values,
    suffix_keys,
    suffix_values,
    new_keys,
    new_values,
    out_weight,
):
    n = lax.axis_size("dp")
    n_kv = lax.axis_size("kv")
    cands, steps, query_width = queries.shape
    kv_width = prefix_keys.shape[2]
    plen = prefix_keys.shape[1]
    depth = suffix_keys.shape[1]
    cols = out_weight.shape[1]
    heads = query_width // HD
    kv_heads = kv_width // HD
    gw = query_width // kv_heads
    rows = cands * steps
    gc = n // n_kv
    cap = max(2, 2 * cands // n)
    slots = -(-cap * steps // 8) * 8
    pad = -(-kv_heads // 8) * 8
    bf16, f32 = jnp.bfloat16, jnp.float32
    smem = pl.BlockSpec(memory_space=pltpu.SMEM)
    vmem = pl.BlockSpec(memory_space=pltpu.VMEM)
    hbm = pl.BlockSpec(memory_space=pl.ANY)
    dma = pltpu.SemaphoreType.DMA

    def by_step(x):
        return jnp.transpose(x, (1, 0, 2)).reshape(rows, x.shape[2])

    out = pl.pallas_call(
        functools.partial(kernel, n, n_kv, cap),
        out_shape=jax.ShapeDtypeStruct((gc, rows, cols), bf16),
        in_specs=[smem] * 2 + [vmem] * 3 + [hbm] * 5,
        out_specs=vmem,
        scratch_shapes=[
            pltpu.VMEM((plen, kv_width), bf16),
            pltpu.VMEM((plen, kv_width), bf16),
            pltpu.VMEM((cands, depth, kv_width), bf16),
            pltpu.VMEM((cands, depth, kv_width), bf16),
            pltpu.VMEM((query_width, cols), bf16),
            pltpu.VMEM((rows * pad, HD), f32),
            pltpu.VMEM((rows * pad, HD), f32),
            pltpu.VMEM((rows * heads, HD), f32),
            pltpu.VMEM((rows * heads, HD), f32),
            pltpu.VMEM((rows * heads, HD), f32),
            pltpu.VMEM((kv_heads, n, slots, gw), bf16),
            pltpu.VMEM((kv_heads, n, slots, gw), bf16),
            pltpu.VMEM((kv_heads, n, slots, gw), bf16),
            pltpu.VMEM((kv_heads, n, 8, HD), f32),
            pltpu.VMEM((kv_heads, n, slots, gw), bf16),
            pltpu.VMEM((kv_heads, n, 8, HD), f32),
            pltpu.VMEM((kv_heads, n, rows, gw), bf16),
            pltpu.VMEM((n, rows, cols), bf16),
            pltpu.VMEM((n_kv, gc, rows, cols), bf16),
            pltpu.VMEM((gc, rows, cols), f32),
            dma((5,)),
            dma((kv_heads, n)),
            dma((kv_heads, n)),
            dma((kv_heads, n)),
            dma((kv_heads, n)),
            dma((kv_heads, n)),
            dma((kv_heads, n)),
            dma((2, kv_heads, n)),
            dma((kv_heads, n)),
            dma((n, cols // min(512, cols))),
            dma((n_kv, gc, cols // min(512, cols))),
        ],
        compiler_params=pltpu.CompilerParams(
            collective_id=0, has_side_effects=True, vmem_limit_bytes=60 * 1024 * 1024
        ),
    )(
        routes.reshape(cands),
        suffix_lengths,
        by_step(queries),
        by_step(new_keys),
        by_step(new_values),
        prefix_keys[0],
        prefix_values[0],
        suffix_keys,
        suffix_values,
        out_weight,
    )
    out = jnp.transpose(out.reshape(gc, steps, cands, cols), (0, 2, 1, 3))
    return out.reshape(gc * cands, steps, cols)


def solution(mesh):
    placed = (
        P(("groups", "dp"), None, "kv"),
        P(("groups", "dp"), None),
        P(("groups", "dp")),
        P(("groups", "dp"), None, "kv"),
        P(("groups", "dp"), None, "kv"),
        P(("groups", "dp"), None, "kv"),
        P(("groups", "dp"), None, "kv"),
        P(("groups", "dp"), None, "kv"),
        P(("groups", "dp"), None, "kv"),
        P("kv", "dp"),
    )
    return jax.shard_map(
        local,
        mesh=mesh,
        in_specs=placed,
        out_specs=P(("groups", "kv"), None, "dp"),
        check_vma=False,
    )
```
